32 devices in a mesh: slab: 4 (over z), blk: 8 (over y, x, core).
Axes of the slice: x: 2, y: 2, z: 4, core: 2. Of those that a mesh axis runs over, the one named last changes fastest.
Arguments:
- voltage: float32 [16, 64, 512], P('slab', 'blk'), may hold values from -1 to 1.2
- voltage_lag: float32 [16, 64, 512], P('slab', 'blk'), may hold values from -1 to 1.2
- tissue: int32 [16, 64, 512], P('slab', 'blk'), may hold values from 0 to 1, as said below
- fiber: int32 [16, 64, 512], P('slab', 'blk'), may hold values from 0 to 15
- conductivity: float32 [6, 16], replicated, may hold values from -0.036 to 0.12, as said below
- worker: int32 [16, 64], P('slab', 'blk'), may hold values from -1 to 127, as said below
- gates: float32 [12, 512, 512], P(None, ('slab', 'blk')), may hold values from 0.02 to 0.98
- gate_half: float32 [12], replicated, may hold values from -0.6 to 0.6
- gate_steep: float32 [12], replicated, may hold values from -8 to 8
- gate_tmin: float32 [12], replicated, may hold values from 0.1 to 0.5
- gate_tspan: float32 [12], replicated, may hold values from 0.2 to 3
- channel: float32 [6], replicated, may hold values from 0.5 to 3
Outputs:
- voltage_out: float32 [16, 64, 512], P('slab', 'blk')
- gates_out: float32 [12, 512, 512], P(None, ('slab', 'blk'))
- charge: float32 [3, 16, 64, 512], P(None, 'slab', 'blk')
The draws below stay inside these ranges and needn't reach their ends.
Inputs may be any that keep to these rules, and one draw needn't show every extreme that they name: `worker`: -1 marks a tile with no tissue. Otherwise the entry is w * 16 + k: the tile's gating variables are row k of the 16 rows of gates held by the device with blk index w in the same slab group. Every such row is named by exactly one tile of its slab group. The tiles of one device name one blk index at most 4 times, and some device does so exactly 4 times. `tissue`: 1 only in tiles whose worker entry is not -1; every such tile holds some tissue. `conductivity`: the first three rows are positive; each class's tensor is positive definite.
All inputs are finite; a program needn't handle non-finite values.
Results may differ from the reference program's by a relative error of at most 0.000088.
Values sent between devices are 32-bit elements; how exact they have to be, the bound alone decides.
A program may use at most 64 MiB of HBM per device.

```python
import math
import jax
import jax.numpy as jnp
from jax import lax

CX = 4
CY = 8
CZ = 512
NG = 12
FIB = 16
STEPS = 3
RCAP = 16
NX = 16
NY = 64
ROWS = 512
N_SLAB = 4
N_BLK = 8


def tissue_layout(key):
    keys = jax.random.split(jax.random.fold_in(key, 11), 5)
    tiles = CX * CY
    group = N_BLK * tiles
    weighting = jax.random.randint(keys[0], (N_SLAB, N_BLK), 0, 4)
    favoured = jax.random.randint(keys[1], (N_SLAB,), 0, N_BLK)
    weighting = jnp.where(jnp.arange(N_BLK)[None, :] == favoured[:, None], 9, weighting)
    noise = jax.random.randint(keys[2], (N_SLAB, group), 0, 4096)
    ranks = jnp.arange(group, dtype=jnp.int32)
    scores = jnp.repeat(weighting, tiles, axis=1) * 67108864 + noise * 16384 + ranks[None, :]
    chosen = lax.top_k(scores, RCAP * N_BLK)[1]
    picked = jnp.zeros((N_SLAB, group), jnp.int32).at[jnp.arange(N_SLAB)[:, None], chosen].set(1)
    order = jnp.cumsum(picked, axis=1) - 1
    targets = jnp.where(picked == 1, order % N_BLK * RCAP + order // N_BLK, -1)
    starts = jax.random.randint(keys[3], (N_SLAB, group), 0, CZ // 4)
    spans = jax.random.randint(keys[4], (N_SLAB, group), CZ // 2, CZ - CZ // 4 + 1)
    depth = jnp.arange(CZ, dtype=jnp.int32)
    inside = (depth >= starts[..., None]) & (depth < starts[..., None] + spans[..., None]) & (picked[..., None] == 1)
    targets = targets.reshape(N_SLAB, N_BLK, CX, CY).transpose(0, 2, 1, 3).reshape(N_SLAB * CX, N_BLK * CY)
    inside = inside.reshape(N_SLAB, N_BLK, CX, CY, CZ).transpose(0, 2, 1, 3, 4).reshape(N_SLAB * CX, N_BLK * CY, CZ)
    return (targets.astype(jnp.int32), inside.astype(jnp.int32))


def draw_worker(key, part):
    return tissue_layout(key)[0]


def draw_tissue(key, part):
    return tissue_layout(key)[1]


def draw_conductivity(key, part):
    keys = jax.random.split(jax.random.fold_in(key, 5), 2)
    lowest, highest, reach = (0.03, 0.1, 0.25)
    diagonal = jnp.exp(jax.random.uniform(keys[0], (3, FIB), jnp.float32, math.log(lowest), math.log(highest)))
    mixing = jax.random.uniform(keys[1], (3, FIB), jnp.float32, -reach, reach)
    products = jnp.stack([diagonal[0] * diagonal[1], diagonal[0] * diagonal[2], diagonal[1] * diagonal[2]])
    return jnp.concatenate([diagonal, mixing * jnp.sqrt(products)], axis=0)


def with_ends(drawn, own_key, low, high):
    place = [jax.random.randint(jax.random.fold_in(own_key, axis), (), 0, length) for axis, length in enumerate(drawn.shape)]
    longest = drawn.shape.index(max(drawn.shape))
    next_to = place[:longest] + [(place[longest] + 1) % drawn.shape[longest]] + place[longest + 1:]
    return drawn.at[tuple(place)].set(low).at[tuple(next_to)].set(high)


def block_scale(own_key, dims, cuts, least, high):
    def one(axis_at, shards_of):
        heights = jax.random.uniform(jax.random.fold_in(jax.random.fold_in(own_key, 6), axis_at), (shards_of,), jnp.float32, least / len(cuts), high / len(cuts))
        return jnp.repeat(jnp.exp(heights), dims[axis_at] // shards_of).reshape((-1,) + (1,) * (len(dims) - axis_at - 1))

    level = one(*cuts[0])
    for cut in cuts[1:]:
        level = level * one(*cut)
    return level


def setup_inputs(seed: int = 0) -> dict:
    seeds = jax.random.split(jax.random.key(seed), 13)
    return {
        "voltage": jnp.clip(-1.0 + 2.2 * jax.random.uniform(seeds[0], (NX, NY, CZ), jnp.float32) ** block_scale(seeds[0], (NX, NY, CZ), ((0, 4), (1, 8)), -0.2, 0.2), -1.0, 1.2),
        "voltage_lag": jnp.clip(-1.0 + 2.2 * jax.random.uniform(seeds[1], (NX, NY, CZ), jnp.float32) ** block_scale(seeds[1], (NX, NY, CZ), ((0, 4), (1, 8)), -0.2, 0.2), -1.0, 1.2),
        "tissue": draw_tissue(jax.random.fold_in(seeds[12], 71), 0),
        "fiber": with_ends(jax.random.randint(seeds[3], (NX, NY, CZ), 0, FIB), jax.random.fold_in(seeds[3], 1), 0, FIB - 1).astype(jnp.int32),
        "conductivity": draw_conductivity(jax.random.fold_in(seeds[12], 71), 0),
        "worker": draw_worker(jax.random.fold_in(seeds[12], 71), 0),
        "gates": jnp.clip(0.02 + 0.96000002 * jax.random.uniform(seeds[6], (NG, ROWS, CZ), jnp.float32) ** block_scale(seeds[6], (NG, ROWS, CZ), ((1, 32),), -0.2, 0.2), 0.02, 0.98),
        "gate_half": jnp.clip(jax.random.uniform(seeds[7], (NG,), jnp.float32, -0.6, 0.6), -0.6, 0.6),
        "gate_steep": jnp.clip(jax.random.uniform(seeds[8], (NG,), jnp.float32, -8.0, 8.0), -8.0, 8.0),
        "gate_tmin": jnp.clip(jnp.exp(jax.random.uniform(seeds[9], (NG,), jnp.float32, math.log(0.1), math.log(0.5))), 0.1, 0.5),
        "gate_tspan": jnp.clip(jnp.exp(jax.random.uniform(seeds[10], (NG,), jnp.float32, math.log(0.2), math.log(3.0))), 0.2, 3.0),
        "channel": jnp.clip(jnp.exp(jax.random.uniform(seeds[11], (6,), jnp.float32, math.log(0.5), math.log(3.0))), 0.5, 3.0),
    }


STEP_DT = 0.1
PHASE_REF = -0.2
PHASE_SOFT = 0.5
COMPONENT = ((1, 4, 5), (4, 2, 6), (5, 6, 3))

def basis(direction, amount):
    return tuple((amount if position == direction else 0 for position in range(3)))

def combine(first, second):
    return tuple((left_part + right_part for left_part, right_part in zip(first, second)))

def window(array, starts, extent):
    leading = array.ndim - 3
    begin = (0,) * leading + tuple(starts)
    finish = tuple(array.shape[:leading]) + tuple((first + count for first, count in zip(starts, extent)))
    return lax.slice(array, begin, finish)

def shifted(array, direction, offset, extent):
    starts = tuple(((0 if position == direction else 1) + offset[position] for position in range(3)))
    sizes = tuple((extent[position] + 1 if position == direction else extent[position] for position in range(3)))
    return window(array, starts, sizes)

def coefficient_stack(weights, fiber, conductivity):
    classes = (fiber[None] == jnp.arange(FIB, dtype=jnp.int32)[:, None, None, None]).astype(jnp.float32)
    sigma = jnp.tensordot(conductivity, classes, axes=(1, 0), precision=lax.Precision.HIGHEST)
    return jnp.concatenate([weights[None], weights[None] * sigma], axis=0)

def face_terms(padded_stack, extent):
    result = []
    for direction in range(3):
        lower = shifted(padded_stack, direction, (0, 0, 0), extent)
        upper = shifted(padded_stack, direction, basis(direction, 1), extent)
        face_mask = lower[0] * upper[0]
        result.append([0.5 * (lower[COMPONENT[direction][other]] + upper[COMPONENT[direction][other]]) * face_mask for other in range(3)])
    return result

def diffuse(padded_field, faces, extent):
    total = jnp.zeros(extent, jnp.float32)
    for direction in range(3):
        along = basis(direction, 1)
        flux = faces[direction][direction] * (shifted(padded_field, direction, along, extent) - shifted(padded_field, direction, (0, 0, 0), extent))
        for other in range(3):
            if other != direction:
                upward = basis(other, 1)
                downward = basis(other, -1)
                slope = (shifted(padded_field, direction, upward, extent) + shifted(padded_field, direction, combine(along, upward), extent) - shifted(padded_field, direction, downward, extent) - shifted(padded_field, direction, combine(along, downward), extent)) * 0.25
                flux = flux + faces[direction][other] * slope
        total = total + jnp.diff(flux, axis=direction)
    return total

def react(potential, states, params):
    gate_half, gate_steep, gate_tmin, gate_tspan, channel = params
    level = potential[None]
    centre = gate_half[:, None, None]
    target = jax.nn.sigmoid(gate_steep[:, None, None] * (level - centre))
    relax = gate_tmin[:, None, None] + gate_tspan[:, None, None] / (1.0 + 4.0 * (level - centre) * (level - centre))
    fresh = target + (states - target) * jnp.exp(-STEP_DT / relax)
    sodium = channel[0] * states[0] * states[0] * states[0] * states[1] * states[2] * (potential - 1.2)
    calcium = channel[1] * states[3] * states[4] * states[5] * states[6] * (potential - 1.0)
    transient = channel[2] * states[7] * states[8] * (potential + 0.9)
    rapid_delayed = channel[3] * states[9] * states[10] * (potential + 0.9)
    slow_delayed = channel[4] * states[11] * states[11] * (potential + 0.8)
    inward_rect = channel[5] * (potential + 0.9) / (1.0 + jnp.exp(4.0 * (potential + 0.6)))
    return (fresh, sodium + calcium + transient + rapid_delayed + slow_delayed + inward_rect)

def edge_term(first, second):
    cross = first[0] * second[1] - first[1] * second[0]
    inner = first[0] * second[0] + first[1] * second[1]
    norm_value = jnp.sqrt((first[0] * first[0] + first[1] * first[1]) * (second[0] * second[0] + second[1] * second[1]))
    return 2.0 * jnp.arctan(cross / (norm_value + inner + PHASE_SOFT))

def charges(padded_phase, extent):
    results = []
    for first_dim, second_dim in ((0, 1), (1, 2), (0, 2)):
        corners = [basis(first_dim, 1), basis(second_dim, 1), basis(first_dim, -1), basis(second_dim, -1)]
        points = [window(padded_phase, tuple((1 + value for value in corner)), extent) for corner in corners]
        circulation = jnp.zeros(extent, jnp.float32)
        for position in range(4):
            circulation = circulation + edge_term(points[position], points[(position + 1) % 4])
        results.append(circulation)
    return jnp.stack(results)

def pad_space(array):
    return jnp.pad(array, [(0, 0)] * (array.ndim - 3) + [(1, 1)] * 3)

def reference(voltage, voltage_lag, tissue, fiber, conductivity, worker, gates, gate_half, gate_steep, gate_tmin, gate_tspan, channel):
    extent = voltage.shape
    params = (gate_half, gate_steep, gate_tmin, gate_tspan, channel)
    weights = tissue.astype(jnp.float32)
    faces = face_terms(pad_space(coefficient_stack(weights, fiber, conductivity)), extent)
    total_rows = N_SLAB * N_BLK * RCAP
    targets = worker.reshape(-1)
    live = targets >= 0
    slab_base = jnp.broadcast_to((jnp.arange(NX, dtype=jnp.int32) // CX * (N_BLK * RCAP))[:, None], (NX, NY)).reshape(-1)
    owned_rows = jnp.where(live, slab_base + targets, total_rows)
    tile_ids = jnp.arange(NX * NY, dtype=jnp.int32)
    tile_of_row = jnp.zeros((total_rows + 1,), jnp.int32).at[owned_rows].set(tile_ids)[:total_rows]
    safe_rows = jnp.minimum(owned_rows, total_rows - 1)
    states = gates
    potential = voltage
    for timestep in range(STEPS):
        tile_volts = potential.reshape(NX * NY, CZ)
        states, row_current = react(tile_volts[tile_of_row], states, params)
        current = jnp.where(live[:, None], row_current[safe_rows], 0.0).reshape(extent)
        spread = diffuse(pad_space(weights * potential), faces, extent)
        potential = potential + weights * (spread - STEP_DT * current)
    phase = jnp.stack([weights * (potential - PHASE_REF), weights * (voltage_lag - PHASE_REF)])
    return (potential, states, charges(pad_space(phase), extent))
```

```python
import functools

import jax
import jax.numpy as jnp
from jax import lax
from jax.experimental import pallas as pl
from jax.experimental.pallas import tpu as pltpu
from jax.sharding import PartitionSpec as P

STEPS = 3
STEP_DT = 0.1
PHASE_REF = -0.2
PHASE_SOFT = 0.5
MESH = pl.DeviceIdType.MESH

FACES = ((-1, 0), (1, 0), (0, -1), (0, 1))
CORNERS = ((-1, -1), (-1, 1), (1, -1), (1, 1))
SIDES = FACES + CORNERS
TISSUE, FIBER, LAG, FINAL = STEPS, STEPS + 1, STEPS + 2, STEPS + 3
EXCHANGES = STEPS + 4


def pick_dot(onehot, values):
    first = values.astype(jnp.bfloat16)
    rest = values - first.astype(jnp.float32)
    second = rest.astype(jnp.bfloat16)
    third = (rest - second.astype(jnp.float32)).astype(jnp.bfloat16)
    dot = functools.partial(jnp.dot, preferred_element_type=jnp.float32)
    return dot(onehot, first) + dot(onehot, second) + dot(onehot, third)


def fold(x, parts):
    width = x.shape[1] // parts
    return jnp.concatenate([x[:, h * width : (h + 1) * width] for h in range(parts)], axis=0)


def unfold(x, parts):
    rows = x.shape[0] // parts
    return jnp.concatenate([x[h * rows : (h + 1) * rows] for h in range(parts)], axis=1)


def edge(p, q):
    cross = p[0] * q[1] - p[1] * q[0]
    den = p[2] * q[2] + (p[0] * q[0] + p[1] * q[1]) + PHASE_SOFT
    num = jnp.abs(cross)
    steep = num > 2.414213562373095 * den
    middle = num > 0.4142135623730950 * den
    top = jnp.where(steep, -den, jnp.where(middle, num - den, num))
    bottom = jnp.where(steep, num, jnp.where(middle, num + den, den))
    base = jnp.where(steep, 1.5707963267948966, jnp.where(middle, 0.7853981633974483, 0.0))
    x = top / bottom
    z = x * x
    poly = ((8.05374449538e-2 * z - 1.38776856032e-1) * z + 1.99777106478e-1) * z - 3.33329491539e-1
    angle = 2.0 * (base + (poly * z * x + x))
    return jnp.where(cross < 0.0, -angle, angle)


def kernel(
    slabs, blocks, cx, cy, depth, gate_count, capacity, pair, parts,
    worker, conductivity, gate_half, gate_steep, gate_tmin, gate_tspan, channel,
    voltage, lag, tissue, fiber, gates,
    volt_out, gates_out, charge,
    hx, hy, hc, sx, sy, sc, ix, iy, iys,
    vsend, vrecv, csend, crecv, clsend, clrecv,
    face_x, face_u, face_l, face_z,
    halo_ss, halo_rs, v_ss, v_rs, c_ss, c_rs, cl_ss, cl_rs,
):
    slab, blk = lax.axis_index("slab"), lax.axis_index("blk")
    tiles = cx * cy
    width = depth // parts

    def exists(side):
        dx, dy = side
        ok = None
        for cond in ([slab > 0] if dx < 0 else [slab < slabs - 1] if dx > 0 else []) + (
            [blk > 0] if dy < 0 else [blk < blocks - 1] if dy > 0 else []
        ):
            ok = cond if ok is None else jnp.logical_and(ok, cond)
        return ok

    def slot(refs, which, side):
        at = SIDES.index(side)
        return refs[0].at[which, at] if at < 2 else refs[1].at[which, at - 2] if at < 4 else refs[2].at[which, at - 4]

    def halo_copy(which, side, src, dst):
        dx, dy = side
        return pltpu.make_async_remote_copy(
            src_ref=src, dst_ref=dst,
            send_sem=halo_ss.at[which, SIDES.index(side)],
            recv_sem=halo_rs.at[which, SIDES.index((-dx, -dy))],
            device_id=(slab + dx, blk + dy), device_id_type=MESH,
        )

    def ring_copy(src, dst, ss, rs, to):
        return pltpu.make_async_remote_copy(
            src_ref=src, dst_ref=dst, send_sem=ss, recv_sem=rs,
            device_id=(slab, to), device_id_type=MESH,
        )

    def ends(which, side):
        opposite = (-side[0], -side[1])
        if which < STEPS or which == FINAL or which == LAG:
            at = which if which < STEPS else STEPS + (which - LAG)
            return slot((sx, sy, sc), at, side), slot((hx, hy, hc), at, opposite)
        ref = tissue if which == TISSUE else fiber
        at = which - TISSUE
        if side[0] != 0:
            return ref.at[0 if side[0] < 0 else cx - 1], slot((ix, iy), at, opposite)
        return iys.at[at, SIDES.index(side) - 2], slot((ix, iy), at, opposite)

    def sides_of(which):
        return SIDES if which < STEPS else FACES

    def start_halo(which):
        for side in sides_of(which):
            @pl.when(exists(side))
            def _():
                halo_copy(which, side, *ends(which, side)).start()

    def wait_halo(which):
        for side in sides_of(which):
            @pl.when(exists(side))
            def _():
                opposite = (-side[0], -side[1])
                src, dst = ends(which, opposite)
                dx, dy = side
                pltpu.make_async_remote_copy(
                    src_ref=src, dst_ref=dst,
                    send_sem=halo_ss.at[which, SIDES.index(side)],
                    recv_sem=halo_rs.at[which, SIDES.index(side)],
                    device_id=(slab + dx, blk + dy), device_id_type=MESH,
                ).wait_recv()

    def wait_sent(which):
        for side in sides_of(which):
            @pl.when(exists(side))
            def _():
                halo_copy(which, side, *ends(which, side)).wait_send()

    for side in SIDES:
        @pl.when(jnp.logical_not(exists(side)))
        def _():
            at = SIDES.index(side)
            ref = hx if at < 2 else hy if at < 4 else hc
            for which in range(STEPS + 2 if at < 4 else STEPS):
                ref[which, at % 2 if at < 4 else at - 4] = jnp.zeros(ref.shape[2:], jnp.float32)
            if at < 4:
                ints = ix if at < 2 else iy
                for which in range(2):
                    ints[which, at % 2] = jnp.zeros(ints.shape[2:], jnp.int32)

    barrier = pltpu.get_barrier_semaphore()
    for d in range(1, blocks):
        pl.semaphore_signal(barrier, inc=1, device_id=(slab, lax.rem(blk + d, blocks)), device_id_type=MESH)
    expected = blocks - 1
    for side in SIDES:
        if side[0] != 0:
            there = exists(side)
            @pl.when(there)
            def _():
                pl.semaphore_signal(barrier, inc=1, device_id=(slab + side[0], blk + side[1]), device_id_type=MESH)
            expected = expected + there.astype(jnp.int32)

    total = blocks * 8
    cols = parts * tiles
    row_iota = lambda shape: lax.broadcasted_iota(jnp.int32, shape, 0)
    lane_iota = lambda shape: lax.broadcasted_iota(jnp.int32, shape, 1)
    lane = lane_iota((1, cols))
    tile_of = lax.rem(lane, tiles)
    part_of = lane // tiles
    target = jnp.zeros((1, cols), jnp.int32)
    for t in range(tiles):
        target = jnp.where(tile_of == t, worker[t // cy, t % cy], target)
    live = target >= 0
    holder = jnp.where(live, target // capacity, -1)
    own_row = jnp.where(live, lax.rem(target, capacity), 0)

    def to_col(row, size):
        square = jnp.broadcast_to(row, (size, size)).astype(jnp.float32)
        same = row_iota((size, size)) == lane_iota((size, size))
        return jnp.sum(jnp.where(same, square, 0.0), axis=1, keepdims=True).astype(jnp.int32)

    holder_col = to_col(holder, cols)[:tiles]
    earlier = (
        (jnp.broadcast_to(holder_col, (tiles, cols)) == jnp.broadcast_to(holder, (tiles, cols)))
        & (row_iota((tiles, cols)) < jnp.broadcast_to(tile_of, (tiles, cols)))
    )
    order = jnp.sum(jnp.where(earlier, 1.0, 0.0), axis=0, keepdims=True).astype(jnp.int32)
    ring = lax.rem(holder - blk + blocks, blocks)
    code = jnp.where(live, ring * 8 + part_of * pair + order, -1)
    pack_mask = row_iota((total, cols)) == jnp.broadcast_to(code, (total, cols))
    pack = jnp.where(pack_mask, 1.0, 0.0).astype(jnp.bfloat16)
    code_col = to_col(code, cols)
    unpack = jnp.where(jnp.broadcast_to(code_col, (cols, total)) == lane_iota((cols, total)), 1.0, 0.0).astype(jnp.bfloat16)
    row_code = jnp.broadcast_to((part_of * capacity + own_row + 1).astype(jnp.float32), (total, cols))
    claim_col = jnp.sum(jnp.where(pack_mask, row_code, 0.0), axis=1, keepdims=True) - 1.0
    clsend[...] = jnp.broadcast_to(claim_col, (total, 128)).reshape(blocks, 8, 128)

    weight = [tissue[x].astype(jnp.float32) for x in range(cx)]
    volts = [voltage[x] for x in range(cx)]

    def send_volts(step):
        slots = pick_dot(pack, fold(jnp.concatenate(volts, axis=0), parts))
        vsend[step] = slots.reshape(blocks, 8, width)
        vrecv[step, 0] = slots[:8]

    def v_copy(step, d):
        return ring_copy(vsend.at[step, d], vrecv.at[step, d], v_ss.at[step, d], v_rs.at[step, d], lax.rem(blk + d, blocks))

    def c_copy(step, d):
        return ring_copy(csend.at[step, d], crecv.at[step, d], c_ss.at[step, d], c_rs.at[step, d], lax.rem(blk - d + blocks, blocks))

    def cl_copy(d):
        return ring_copy(clsend.at[d], clrecv.at[d], cl_ss.at[d], cl_rs.at[d], lax.rem(blk + d, blocks))

    def stage(planes, at, corners):
        sx[at, 0] = planes[0]
        sx[at, 1] = planes[cx - 1]
        for end, y in ((0, 0), (1, cy - 1)):
            sy[at, end] = jnp.concatenate([planes[x][y : y + 1] for x in range(cx)], axis=0)
        if corners:
            for i, (dx, dy) in enumerate(CORNERS):
                y = 0 if dy < 0 else cy - 1
                sc[at, i] = planes[0 if dx < 0 else cx - 1][y : y + 1]

    for at, ref in ((0, tissue), (1, fiber)):
        for end, y in ((0, 0), (1, cy - 1)):
            iys[at, end] = jnp.concatenate([ref[x, y : y + 1] for x in range(cx)], axis=0)
    send_volts(0)
    clrecv[0] = clsend[0]
    field = [weight[x] * volts[x] for x in range(cx)]
    stage(field, 0, True)
    phase_b = [weight[x] * (lag[x] - PHASE_REF) for x in range(cx)]
    stage(phase_b, STEPS, False)

    pl.semaphore_wait(barrier, expected)
    for d in range(1, blocks):
        cl_copy(d).start()
        v_copy(0, d).start()
    start_halo(TISSUE)
    start_halo(FIBER)
    start_halo(0)
    start_halo(LAG)

    plane = (cy, depth)
    sub = lax.broadcasted_iota(jnp.int32, plane, 0)
    zlane = lax.broadcasted_iota(jnp.int32, plane, 1)

    def up_y(x, row):
        return jnp.where(sub == cy - 1, jnp.broadcast_to(row, plane), pltpu.roll(x, cy - 1, 0))

    def down_y(x, row):
        return jnp.where(sub == 0, jnp.broadcast_to(row, plane), pltpu.roll(x, 1, 0))

    def wrap_up(x):
        return pltpu.roll(x, depth - 1, 1)

    def wrap_down(x):
        return pltpu.roll(x, 1, 1)

    def up_z(x):
        return jnp.where(zlane == depth - 1, 0.0, wrap_up(x))

    def down_z(x):
        return jnp.where(zlane == 0, 0.0, wrap_down(x))

    wait_halo(TISSUE)
    wait_halo(FIBER)

    def sigma(classes, component):
        table = [conductivity[component, i] for i in range(conductivity.shape[1])]
        out = jnp.full(classes.shape, table[0], jnp.float32)
        for i in range(1, len(table)):
            out = jnp.where(classes == i, table[i], out)
        return out

    kinds = [fiber[x] for x in range(cx)]
    w_lo, w_hi = ix[0, 0].astype(jnp.float32), ix[0, 1].astype(jnp.float32)
    wy_lo, wy_hi = iy[0, 0].astype(jnp.float32), iy[0, 1].astype(jnp.float32)
    for component, spots in ((0, "x"), (1, "y"), (2, "z"), (3, "xy"), (4, "xz"), (5, "yz")):
        own = [sigma(kinds[x], component) for x in range(cx)]
        scale = lambda d: 0.5 if component == "xyz".index(d) else 0.125
        other = {"x": 0, "y": 1, "z": 2}
        def place(d):
            rest = [c for c in spots if c != d]
            return other[rest[0]] if rest else other[d]
        if "x" in spots:
            s = [sigma(ix[1, 0], component)] + own + [sigma(ix[1, 1], component)]
            w = [w_lo] + weight + [w_hi]
            for x in range(cx + 1):
                face_x[place("x"), x] = scale("x") * (s[x] + s[x + 1]) * (w[x] * w[x + 1])
        if "y" in spots:
            low, high = sigma(iy[1, 0], component), sigma(iy[1, 1], component)
            for x in range(cx):
                face_u[place("y"), x] = scale("y") * (own[x] + up_y(own[x], high[x : x + 1])) * (weight[x] * up_y(weight[x], wy_hi[x : x + 1]))
                face_l[place("y"), x] = scale("y") * (own[x] + down_y(own[x], low[x : x + 1])) * (weight[x] * down_y(weight[x], wy_lo[x : x + 1]))
        if "z" in spots:
            for x in range(cx):
                face_z[place("z"), x] = scale("z") * (own[x] + wrap_up(own[x])) * (weight[x] * up_z(weight[x]))

    def spread(field, step):
        f0 = [hx[step, 0]] + field + [hx[step, 1]]
        y_lo, y_hi = hy[step, 0], hy[step, 1]
        rows_lo = [hc[step, 0]] + [y_lo[x : x + 1] for x in range(cx)] + [hc[step, 2]]
        rows_hi = [hc[step, 1]] + [y_hi[x : x + 1] for x in range(cx)] + [hc[step, 3]]
        fu = [up_y(f0[i], rows_hi[i]) for i in range(cx + 2)]
        fd = [down_y(f0[i], rows_lo[i]) for i in range(cx + 2)]
        dy = [fu[i] - fd[i] for i in range(cx + 2)]
        up0 = [up_z(f) for f in f0]
        dz = [up0[i] - down_z(f0[i]) for i in range(cx + 2)]
        z_lo, z_hi = {}, {}
        flux_x = [
            face_x[0, i] * (f0[i + 1] - f0[i]) + face_x[1, i] * (dy[i] + dy[i + 1]) + face_x[2, i] * (dz[i] + dz[i + 1])
            for i in range(cx + 1)
        ]
        result = []
        for x in range(cx):
            i = x + 1
            dx, dxu, dxd = f0[i + 1] - f0[i - 1], fu[i + 1] - fu[i - 1], fd[i + 1] - fd[i - 1]
            dzu, dzd = up_z(fu[i]) - down_z(fu[i]), up_z(fd[i]) - down_z(fd[i])
            flux_u = face_u[1, x] * (fu[i] - f0[i]) + face_u[0, x] * (dx + dxu) + face_u[2, x] * (dz[i] + dzu)
            flux_l = face_l[1, x] * (f0[i] - fd[i]) + face_l[0, x] * (dx + dxd) + face_l[2, x] * (dz[i] + dzd)
            flux_z = (
                face_z[2, x] * (up0[i] - f0[i])
                + face_z[0, x] * (dx + wrap_up(dx))
                + face_z[1, x] * (dy[i] + wrap_up(dy[i]))
            )
            result.append((flux_x[i] - flux_x[i - 1]) + (flux_u - flux_l) + (flux_z - wrap_down(flux_z)))
        return result

    for step in range(STEPS):
        states = gates if step == 0 else gates_out
        if step == 0:
            for d in range(1, blocks):
                cl_copy(d).wait_recv()
            claims = clrecv[...].reshape(total, 128)
            picks = parts * capacity
            claim = claims[:, :1].astype(jnp.int32)
            give = jnp.where(jnp.broadcast_to(claim, (total, picks)) == lane_iota((total, picks)), 1.0, 0.0).astype(jnp.bfloat16)
            same = row_iota((total, total)) == lane_iota((total, total))
            claim_row = jnp.sum(
                jnp.where(same, jnp.broadcast_to(claims[:, :1], (total, total)), 0.0), axis=0, keepdims=True
            ).astype(jnp.int32)
            take = jnp.where(row_iota((picks, total)) == jnp.broadcast_to(claim_row, (picks, total)), 1.0, 0.0).astype(jnp.bfloat16)
        for d in range(1, blocks):
            v_copy(step, d).wait_recv()
        v = unfold(pick_dot(take, vrecv[step].reshape(total, width)), parts)
        s = [states[g] for g in range(12)]
        current = (
            channel[0] * s[0] * s[0] * s[0] * s[1] * s[2] * (v - 1.2)
            + channel[1] * s[3] * s[4] * s[5] * s[6] * (v - 1.0)
            + channel[2] * s[7] * s[8] * (v + 0.9)
            + channel[3] * s[9] * s[10] * (v + 0.9)
            + channel[4] * s[11] * s[11] * (v + 0.8)
            + channel[5] * (v + 0.9) / (1.0 + jnp.exp(4.0 * (v + 0.6)))
        )
        back = pick_dot(give, fold(current, parts))
        csend[step] = back.reshape(blocks, 8, width)
        crecv[step, 0] = back[:8]
        for d in range(1, blocks):
            c_copy(step, d).start()
        for g in range(gate_count):
            off = v - gate_half[g]
            goal = 1.0 / (1.0 + jnp.exp(-gate_steep[g] * off))
            quad = 1.0 + 4.0 * off * off
            decay = jnp.exp((-STEP_DT * quad) / (gate_tmin[g] * quad + gate_tspan[g]))
            gates_out[g] = goal + (states[g] - goal) * decay
        wait_halo(step)
        moved = spread(field, step)
        for d in range(1, blocks):
            c_copy(step, d).wait_recv()
        drain = unfold(pick_dot(unpack, crecv[step].reshape(total, width)), parts)
        volts = [
            volts[x] + weight[x] * (moved[x] - STEP_DT * drain[x * cy : (x + 1) * cy])
            for x in range(cx)
        ]
        if step < STEPS - 1:
            send_volts(step + 1)
            for d in range(1, blocks):
                v_copy(step + 1, d).start()
            field = [weight[x] * volts[x] for x in range(cx)]
            stage(field, step + 1, True)
            start_halo(step + 1)

    phase_a = [weight[x] * (volts[x] - PHASE_REF) for x in range(cx)]
    stage(phase_a, STEPS + 1, False)
    start_halo(FINAL)
    for x in range(cx):
        volt_out[x] = volts[x]
    wait_halo(LAG)
    wait_halo(FINAL)

    def length(a, b):
        return jnp.sqrt(a * a + b * b)

    A, B = STEPS + 1, STEPS
    points = [(phase_a[x], phase_b[x], length(phase_a[x], phase_b[x])) for x in range(cx)]
    outer = [(hx[A, e], hx[B, e], length(hx[A, e], hx[B, e])) for e in range(2)]
    rim = [(hy[A, e], hy[B, e], length(hy[A, e], hy[B, e])) for e in range(2)]
    line = [outer[0]] + points + [outer[1]]
    for x in range(cx):
        here = points[x]
        xu, xd = line[x + 2], line[x]
        yu = tuple(up_y(here[k], rim[1][k][x : x + 1]) for k in range(3))
        yd = tuple(down_y(here[k], rim[0][k][x : x + 1]) for k in range(3))
        zu = tuple(up_z(here[k]) for k in range(3))
        zd = tuple(down_z(here[k]) for k in range(3))
        for k, (p0, p1, p2, p3) in enumerate(((xu, yu, xd, yd), (yu, zu, yd, zd), (xu, zu, xd, zd))):
            charge[k, x] = edge(p0, p1) + edge(p1, p2) + edge(p2, p3) + edge(p3, p0)

    for which in range(EXCHANGES):
        wait_sent(which)
    for d in range(1, blocks):
        cl_copy(d).wait_send()
        for step in range(STEPS):
            v_copy(step, d).wait_send()
            c_copy(step, d).wait_send()


def on_device(
    voltage, voltage_lag, tissue, fiber, conductivity, worker, gates,
    gate_half, gate_steep, gate_tmin, gate_tspan, channel,
):
    cx, cy, depth = voltage.shape
    gate_count, capacity, _ = gates.shape
    slabs, blocks = lax.axis_size("slab"), lax.axis_size("blk")
    pair = max(1, cx * cy // blocks)
    parts = max(1, min(8 // pair, depth // 128))
    width = depth // parts
    f32, i32 = jnp.float32, jnp.int32
    halos = STEPS + 2
    smem = pl.BlockSpec(memory_space=pltpu.SMEM)
    vmem = pl.BlockSpec(memory_space=pltpu.VMEM)
    dma = pltpu.SemaphoreType.DMA
    return pl.pallas_call(
        functools.partial(kernel, slabs, blocks, cx, cy, depth, gate_count, capacity, pair, parts),
        out_shape=(
            jax.ShapeDtypeStruct(voltage.shape, f32),
            jax.ShapeDtypeStruct(gates.shape, f32),
            jax.ShapeDtypeStruct((3,) + voltage.shape, f32),
        ),
        in_specs=[smem] * 7 + [vmem] * 5,
        out_specs=(vmem, vmem, vmem),
        scratch_shapes=[
            pltpu.VMEM((halos, 2, cy, depth), f32),
            pltpu.VMEM((halos, 2, cx, depth), f32),
            pltpu.VMEM((STEPS, 4, 1, depth), f32),
            pltpu.VMEM((halos, 2, cy, depth), f32),
            pltpu.VMEM((halos, 2, cx, depth), f32),
            pltpu.VMEM((STEPS, 4, 1, depth), f32),
            pltpu.VMEM((2, 2, cy, depth), i32),
            pltpu.VMEM((2, 2, cx, depth), i32),
            pltpu.VMEM((2, 2, cx, depth), i32),
            pltpu.VMEM((STEPS, blocks, 8, width), f32),
            pltpu.VMEM((STEPS, blocks, 8, width), f32),
            pltpu.VMEM((STEPS, blocks, 8, width), f32),
            pltpu.VMEM((STEPS, blocks, 8, width), f32),
            pltpu.VMEM((blocks, 8, 128), f32),
            pltpu.VMEM((blocks, 8, 128), f32),
            pltpu.VMEM((3, cx + 1, cy, depth), f32),
            pltpu.VMEM((3, cx, cy, depth), f32),
            pltpu.VMEM((3, cx, cy, depth), f32),
            pltpu.VMEM((3, cx, cy, depth), f32),
            dma((EXCHANGES, 8)), dma((EXCHANGES, 8)),
            dma((STEPS, blocks)), dma((STEPS, blocks)),
            dma((STEPS, blocks)), dma((STEPS, blocks)),
            dma((blocks,)), dma((blocks,)),
        ],
        compiler_params=pltpu.CompilerParams(collective_id=0, has_side_effects=True),
        name="steps",
    )(
        worker, conductivity, gate_half, gate_steep, gate_tmin, gate_tspan, channel,
        voltage, voltage_lag, tissue, fiber, gates,
    )


def solution(mesh):
    grid = P("slab", "blk", None)
    in_specs = (
        grid, grid, grid, grid, P(), P("slab", "blk"), P(None, ("slab", "blk"), None),
        P(), P(), P(), P(), P(),
    )
    out_specs = (grid, P(None, ("slab", "blk"), None), P(None, "slab", "blk", None))
    return jax.shard_map(on_device, mesh=mesh, in_specs=in_specs, out_specs=out_specs, check_vma=False)
```

```python
import functools

import jax
import jax.numpy as jnp
from jax import lax
from jax.experimental import pallas as pl
from jax.experimental.pallas import tpu as pltpu
from jax.sharding import PartitionSpec as P

STEPS = 3
STEP_DT = 0.1
PHASE_REF = -0.2
PHASE_SOFT = 0.5
MESH = pl.DeviceIdType.MESH

FACES = ((-1, 0), (1, 0), (0, -1), (0, 1))
CORNERS = ((-1, -1), (-1, 1), (1, -1), (1, 1))
SIDES = FACES + CORNERS
TISSUE, FIBER, LAG, FINAL = STEPS, STEPS + 1, STEPS + 2, STEPS + 3
EXCHANGES = STEPS + 4


def pick_dot(onehot, values):
    first = values.astype(jnp.bfloat16)
    rest = values - first.astype(jnp.float32)
    second = rest.astype(jnp.bfloat16)
    third = (rest - second.astype(jnp.float32)).astype(jnp.bfloat16)
    dot = functools.partial(jnp.dot, preferred_element_type=jnp.float32)
    return dot(onehot, first) + dot(onehot, second) + dot(onehot, third)


def fold(x, parts):
    width = x.shape[1] // parts
    return jnp.concatenate([x[:, h * width : (h + 1) * width] for h in range(parts)], axis=0)


def unfold(x, parts):
    rows = x.shape[0] // parts
    return jnp.concatenate([x[h * rows : (h + 1) * rows] for h in range(parts)], axis=1)


def edge(p, q):
    cross = p[0] * q[1] - p[1] * q[0]
    den = p[2] * q[2] + (p[0] * q[0] + p[1] * q[1]) + PHASE_SOFT
    num = jnp.abs(cross)
    steep = num > 2.414213562373095 * den
    middle = num > 0.4142135623730950 * den
    top = jnp.where(steep, -den, jnp.where(middle, num - den, num))
    bottom = jnp.where(steep, num, jnp.where(middle, num + den, den))
    base = jnp.where(steep, 1.5707963267948966, jnp.where(middle, 0.7853981633974483, 0.0))
    x = top / bottom
    z = x * x
    poly = ((8.05374449538e-2 * z - 1.38776856032e-1) * z + 1.99777106478e-1) * z - 3.33329491539e-1
    angle = 2.0 * (base + (poly * z * x + x))
    return jnp.where(cross < 0.0, -angle, angle)


def kernel(
    slabs, blocks, cx, cy, depth, gate_count, capacity, pair, parts,
    worker, conductivity, gate_half, gate_steep, gate_tmin, gate_tspan, channel,
    voltage_in, lag_in, tissue_in, fiber_in, gates_in,
    volt_out, gates_out, charge,
    voltage, lag, tissue, fiber, gates,
    hx, hy, hc, sx, sy, sc, ix, iy, iys,
    vsend, vrecv, csend, crecv, clsend, clrecv,
    sig, face_x, face_u, face_l, face_z,
    in_s, halo_ss, halo_rs, v_ss, v_rs, c_ss, c_rs, cl_ss, cl_rs,
):
    slab, blk = lax.axis_index("slab"), lax.axis_index("blk")
    tiles = cx * cy
    width = depth // parts
    loads = [
        pltpu.make_async_copy(src, dst, in_s.at[i])
        for i, (src, dst) in enumerate((
            (voltage_in, voltage), (tissue_in, tissue), (fiber_in, fiber), (lag_in, lag), (gates_in, gates),
        ))
    ]
    for load in loads:
        load.start()

    def exists(side):
        dx, dy = side
        ok = None
        for cond in ([slab > 0] if dx < 0 else [slab < slabs - 1] if dx > 0 else []) + (
            [blk > 0] if dy < 0 else [blk < blocks - 1] if dy > 0 else []
        ):
            ok = cond if ok is None else jnp.logical_and(ok, cond)
        return ok

    def slot(refs, which, side):
        at = SIDES.index(side)
        return refs[0].at[which, at] if at < 2 else refs[1].at[which, at - 2] if at < 4 else refs[2].at[which, at - 4]

    def halo_copy(which, side, src, dst):
        dx, dy = side
        return pltpu.make_async_remote_copy(
            src_ref=src, dst_ref=dst,
            send_sem=halo_ss.at[which, SIDES.index(side)],
            recv_sem=halo_rs.at[which, SIDES.index((-dx, -dy))],
            device_id=(slab + dx, blk + dy), device_id_type=MESH,
        )

    def ring_copy(src, dst, ss, rs, to):
        return pltpu.make_async_remote_copy(
            src_ref=src, dst_ref=dst, send_sem=ss, recv_sem=rs,
            device_id=(slab, to), device_id_type=MESH,
        )

    def ends(which, side):
        opposite = (-side[0], -side[1])
        if which < STEPS or which == FINAL or which == LAG:
            at = which if which < STEPS else STEPS + (which - LAG)
            return slot((sx, sy, sc), at, side), slot((hx, hy, hc), at, opposite)
        ref = tissue if which == TISSUE else fiber
        at = which - TISSUE
        if side[0] != 0:
            return ref.at[0 if side[0] < 0 else cx - 1], slot((ix, iy), at, opposite)
        return iys.at[at, SIDES.index(side) - 2], slot((ix, iy), at, opposite)

    def sides_of(which):
        return SIDES if which < STEPS else FACES

    def start_halo(which):
        for side in sides_of(which):
            @pl.when(exists(side))
            def _():
                halo_copy(which, side, *ends(which, side)).start()

    def wait_halo(which):
        for side in sides_of(which):
            @pl.when(exists(side))
            def _():
                opposite = (-side[0], -side[1])
                src, dst = ends(which, opposite)
                dx, dy = side
                pltpu.make_async_remote_copy(
                    src_ref=src, dst_ref=dst,
                    send_sem=halo_ss.at[which, SIDES.index(side)],
                    recv_sem=halo_rs.at[which, SIDES.index(side)],
                    device_id=(slab + dx, blk + dy), device_id_type=MESH,
                ).wait_recv()

    def wait_sent(which):
        for side in sides_of(which):
            @pl.when(exists(side))
            def _():
                halo_copy(which, side, *ends(which, side)).wait_send()

    for side in SIDES:
        @pl.when(jnp.logical_not(exists(side)))
        def _():
            at = SIDES.index(side)
            ref = hx if at < 2 else hy if at < 4 else hc
            for which in range(STEPS + 2 if at < 4 else STEPS):
                ref[which, at % 2 if at < 4 else at - 4] = jnp.zeros(ref.shape[2:], jnp.float32)
            if at < 4:
                ints = ix if at < 2 else iy
                for which in range(2):
                    ints[which, at % 2] = jnp.zeros(ints.shape[2:], jnp.int32)

    barrier = pltpu.get_barrier_semaphore()
    for d in range(1, blocks):
        pl.semaphore_signal(barrier, inc=1, device_id=(slab, lax.rem(blk + d, blocks)), device_id_type=MESH)
    expected = blocks - 1
    for side in SIDES:
        if side[0] != 0:
            there = exists(side)
            @pl.when(there)
            def _():
                pl.semaphore_signal(barrier, inc=1, device_id=(slab + side[0], blk + side[1]), device_id_type=MESH)
            expected = expected + there.astype(jnp.int32)

    total = blocks * 8
    cols = parts * tiles
    row_iota = lambda shape: lax.broadcasted_iota(jnp.int32, shape, 0)
    lane_iota = lambda shape: lax.broadcasted_iota(jnp.int32, shape, 1)
    lane = lane_iota((1, cols))
    tile_of = lax.rem(lane, tiles)
    part_of = lane // tiles
    target = jnp.zeros((1, cols), jnp.int32)
    for t in range(tiles):
        target = jnp.where(tile_of == t, worker[t // cy, t % cy], target)
    live = target >= 0
    holder = jnp.where(live, target // capacity, -1)
    own_row = jnp.where(live, lax.rem(target, capacity), 0)

    def to_col(row, size):
        square = jnp.broadcast_to(row, (size, size)).astype(jnp.float32)
        same = row_iota((size, size)) == lane_iota((size, size))
        return jnp.sum(jnp.where(same, square, 0.0), axis=1, keepdims=True).astype(jnp.int32)

    holder_col = to_col(holder, cols)[:tiles]
    earlier = (
        (jnp.broadcast_to(holder_col, (tiles, cols)) == jnp.broadcast_to(holder, (tiles, cols)))
        & (row_iota((tiles, cols)) < jnp.broadcast_to(tile_of, (tiles, cols)))
    )
    order = jnp.sum(jnp.where(earlier, 1.0, 0.0), axis=0, keepdims=True).astype(jnp.int32)
    ring = lax.rem(holder - blk + blocks, blocks)
    code = jnp.where(live, ring * 8 + part_of * pair + order, -1)
    pack_mask = row_iota((total, cols)) == jnp.broadcast_to(code, (total, cols))
    pack = jnp.where(pack_mask, 1.0, 0.0).astype(jnp.bfloat16)
    code_col = to_col(code, cols)
    unpack = jnp.where(jnp.broadcast_to(code_col, (cols, total)) == lane_iota((cols, total)), 1.0, 0.0).astype(jnp.bfloat16)
    row_code = jnp.broadcast_to((part_of * capacity + own_row + 1).astype(jnp.float32), (total, cols))
    claim_col = jnp.sum(jnp.where(pack_mask, row_code, 0.0), axis=1, keepdims=True) - 1.0
    clsend[:, :, :128] = jnp.broadcast_to(claim_col, (total, 128)).reshape(blocks, 8, 128)

    loads[0].wait()
    loads[1].wait()
    weight = [tissue[x].astype(jnp.float32) for x in range(cx)]
    volts = [voltage[x] for x in range(cx)]

    def send_rows(step, planes):
        slots = pick_dot(pack, fold(jnp.concatenate(planes, axis=0), parts))
        vsend[step] = slots.reshape(blocks, 8, width)
        vrecv[step, 0] = slots[:8]

    def v_copy(step, d):
        return ring_copy(vsend.at[step, d], vrecv.at[step, d], v_ss.at[step], v_rs.at[step], lax.rem(blk + d, blocks))

    def c_copy(step, d):
        return ring_copy(csend.at[step, d], crecv.at[step, d], c_ss.at[step], c_rs.at[step], lax.rem(blk - d + blocks, blocks))

    def cl_copy(d):
        return ring_copy(clsend.at[d], clrecv.at[d], cl_ss, cl_rs, lax.rem(blk + d, blocks))

    rest = pl.ds(1, blocks - 1)
    after = lax.rem(blk + 1, blocks)

    def v_all(step):
        return ring_copy(vsend.at[step, rest], vrecv.at[step, rest], v_ss.at[step], v_rs.at[step], after)

    def c_all(step):
        return ring_copy(csend.at[step, rest], crecv.at[step, rest], c_ss.at[step], c_rs.at[step], after)

    def cl_all():
        return ring_copy(clsend.at[rest], clrecv.at[rest], cl_ss, cl_rs, after)

    def stage(planes, at, corners):
        sx[at, 0] = planes[0]
        sx[at, 1] = planes[cx - 1]
        for end, y in ((0, 0), (1, cy - 1)):
            sy[at, end] = jnp.concatenate([planes[x][y : y + 1] for x in range(cx)], axis=0)
        if corners:
            for i, (dx, dy) in enumerate(CORNERS):
                y = 0 if dy < 0 else cy - 1
                sc[at, i] = planes[0 if dx < 0 else cx - 1][y : y + 1]

    send_rows(0, volts)
    bit_rows = fold(jnp.concatenate(weight, axis=0), parts).astype(jnp.bfloat16)
    clsend[:, :, 128:] = jnp.dot(pack, bit_rows, preferred_element_type=jnp.float32).reshape(blocks, 8, width)
    clrecv[0] = clsend[0]
    field = [weight[x] * volts[x] for x in range(cx)]
    stage(field, 0, True)
    loads[2].wait()
    for at, ref in ((0, tissue), (1, fiber)):
        for end, y in ((0, 0), (1, cy - 1)):
            iys[at, end] = jnp.concatenate([ref[x, y : y + 1] for x in range(cx)], axis=0)

    pl.semaphore_wait(barrier, expected)
    for d in range(1, blocks):
        v_copy(0, d).start()
        cl_copy(d).start()
    start_halo(0)
    start_halo(TISSUE)
    start_halo(FIBER)
    loads[3].wait()
    phase_b = [weight[x] * (lag[x] - PHASE_REF) for x in range(cx)]
    stage(phase_b, STEPS, False)
    start_halo(LAG)

    plane = (cy, depth)
    sub = lax.broadcasted_iota(jnp.int32, plane, 0)
    zlane = lax.broadcasted_iota(jnp.int32, plane, 1)
    row_zlane = lax.broadcasted_iota(jnp.int32, (cx, depth), 1)

    def up_y(x, row):
        return jnp.where(sub == cy - 1, jnp.broadcast_to(row, plane), pltpu.roll(x, cy - 1, 0))

    def down_y(x, row):
        return jnp.where(sub == 0, jnp.broadcast_to(row, plane), pltpu.roll(x, 1, 0))

    def wrap_up(x):
        return pltpu.roll(x, depth - 1, 1)

    def wrap_down(x):
        return pltpu.roll(x, 1, 1)

    def up_z(x):
        return jnp.where(zlane == depth - 1, 0.0, wrap_up(x))

    def down_z(x):
        return jnp.where(zlane == 0, 0.0, wrap_down(x))

    def sigma(classes, component):
        table = [conductivity[component, i] for i in range(conductivity.shape[1])]
        out = jnp.full(classes.shape, table[0], jnp.float32)
        for i in range(1, len(table)):
            out = jnp.where(classes == i, table[i], out)
        return out

    names = ("x", "y", "z", "xy", "xz", "yz")

    def place(spots, d):
        others = [c for c in spots if c != d]
        return "xyz".index(others[0] if others else d)

    def scale(spots):
        return 0.5 if len(spots) == 1 else 0.125

    for component, spots in enumerate(names):
        own = [sigma(fiber[x], component) for x in range(cx)]
        for x in range(cx):
            sig[component, x] = own[x]
        if "x" in spots:
            for x in range(1, cx):
                face_x[place(spots, "x"), x] = scale(spots) * (own[x - 1] + own[x]) * (weight[x - 1] * weight[x])
        if "z" in spots:
            for x in range(cx):
                face_z[place(spots, "z"), x] = scale(spots) * (own[x] + wrap_up(own[x])) * (weight[x] * up_z(weight[x]))

    def outer_faces():
        w_lo, w_hi = ix[0, 0].astype(jnp.float32), ix[0, 1].astype(jnp.float32)
        wy_lo, wy_hi = iy[0, 0].astype(jnp.float32), iy[0, 1].astype(jnp.float32)
        both_u = [weight[x] * up_y(weight[x], wy_hi[x : x + 1]) for x in range(cx)]
        both_l = [weight[x] * down_y(weight[x], wy_lo[x : x + 1]) for x in range(cx)]
        for component, spots in enumerate(names):
            if "x" in spots:
                at = place(spots, "x")
                face_x[at, 0] = scale(spots) * (sigma(ix[1, 0], component) + sig[component, 0]) * (w_lo * weight[0])
                face_x[at, cx] = scale(spots) * (sig[component, cx - 1] + sigma(ix[1, 1], component)) * (weight[cx - 1] * w_hi)
            if "y" in spots:
                at = place(spots, "y")
                low, high = sigma(iy[1, 0], component), sigma(iy[1, 1], component)
                for x in range(cx):
                    mine = sig[component, x]
                    face_u[at, x] = scale(spots) * (mine + up_y(mine, high[x : x + 1])) * both_u[x]
                    face_l[at, x] = scale(spots) * (mine + down_y(mine, low[x : x + 1])) * both_l[x]

    def spread(field, step):
        f0 = [hx[step, 0]] + field + [hx[step, 1]]
        y_lo, y_hi = hy[step, 0], hy[step, 1]
        rows_lo = [hc[step, 0]] + [y_lo[x : x + 1] for x in range(cx)] + [hc[step, 2]]
        rows_hi = [hc[step, 1]] + [y_hi[x : x + 1] for x in range(cx)] + [hc[step, 3]]
        fu = [up_y(f0[i], rows_hi[i]) for i in range(cx + 2)]
        fd = [down_y(f0[i], rows_lo[i]) for i in range(cx + 2)]
        dy = [fu[i] - fd[i] for i in range(cx + 2)]
        up0 = [up_z(f) for f in f0]
        dz = [up0[i] - down_z(f0[i]) for i in range(cx + 2)]
        z_lo, z_hi = {}, {}
        flux_x = [
            face_x[0, i] * (f0[i + 1] - f0[i]) + face_x[1, i] * (dy[i] + dy[i + 1]) + face_x[2, i] * (dz[i] + dz[i + 1])
            for i in range(cx + 1)
        ]
        result = []
        for x in range(cx):
            i = x + 1
            dx, dxu, dxd = f0[i + 1] - f0[i - 1], fu[i + 1] - fu[i - 1], fd[i + 1] - fd[i - 1]
            dzu, dzd = up_z(fu[i]) - down_z(fu[i]), up_z(fd[i]) - down_z(fd[i])
            flux_u = face_u[1, x] * (fu[i] - f0[i]) + face_u[0, x] * (dx + dxu) + face_u[2, x] * (dz[i] + dzu)
            flux_l = face_l[1, x] * (f0[i] - fd[i]) + face_l[0, x] * (dx + dxd) + face_l[2, x] * (dz[i] + dzd)
            flux_z = (
                face_z[2, x] * (up0[i] - f0[i])
                + face_z[0, x] * (dx + wrap_up(dx))
                + face_z[1, x] * (dy[i] + wrap_up(dy[i]))
            )
            result.append((flux_x[i] - flux_x[i - 1]) + (flux_u - flux_l) + (flux_z - wrap_down(flux_z)))
        return result

    for step in range(STEPS):
        states = gates if step == 0 else gates_out
        if step == 0:
            v_all(0).wait_recv()
            cl_all().wait_recv()
            claims = clrecv[:, :, :128].reshape(total, 128)
            picks = parts * capacity
            claim = claims[:, :1].astype(jnp.int32)
            give = jnp.where(jnp.broadcast_to(claim, (total, picks)) == lane_iota((total, picks)), 1.0, 0.0).astype(jnp.bfloat16)
            same = row_iota((total, total)) == lane_iota((total, total))
            claim_row = jnp.sum(
                jnp.where(same, jnp.broadcast_to(claims[:, :1], (total, total)), 0.0), axis=0, keepdims=True
            ).astype(jnp.int32)
            take = jnp.where(row_iota((picks, total)) == jnp.broadcast_to(claim_row, (picks, total)), 1.0, 0.0).astype(jnp.bfloat16)
            bits = clrecv[:, :, 128:].reshape(total, width).astype(jnp.bfloat16)
            row_weight = unfold(jnp.dot(take, bits, preferred_element_type=jnp.float32), parts)
            loads[4].wait()
        else:
            v_all(step).wait_recv()
        arrived = unfold(pick_dot(take, vrecv[step].reshape(total, width)), parts)
        v = v + row_weight * (arrived - STEP_DT * current) if step == 1 else arrived
        s = [states[g] for g in range(12)]
        current = (
            channel[0] * s[0] * s[0] * s[0] * s[1] * s[2] * (v - 1.2)
            + channel[1] * s[3] * s[4] * s[5] * s[6] * (v - 1.0)
            + channel[2] * s[7] * s[8] * (v + 0.9)
            + channel[3] * s[9] * s[10] * (v + 0.9)
            + channel[4] * s[11] * s[11] * (v + 0.8)
            + channel[5] * (v + 0.9) / (1.0 + jnp.exp(4.0 * (v + 0.6)))
        )
        back = pick_dot(give, fold(current, parts))
        csend[step] = back.reshape(blocks, 8, width)
        crecv[step, 0] = back[:8]
        for d in range(1, blocks):
            c_copy(step, d).start()
        if step == 0:
            wait_halo(TISSUE)
            wait_halo(FIBER)
            outer_faces()
            wait_halo(0)
            moved = spread(field, 0)
            send_rows(1, moved)
            for d in range(1, blocks):
                v_copy(1, d).start()
        for g in range(gate_count):
            off = v - gate_half[g]
            goal = 1.0 / (1.0 + jnp.exp(-gate_steep[g] * off))
            quad = 1.0 + 4.0 * off * off
            decay = jnp.exp((-STEP_DT * quad) / (gate_tmin[g] * quad + gate_tspan[g]))
            gates_out[g] = goal + (states[g] - goal) * decay
        if step > 0:
            wait_halo(step)
            moved = spread(field, step)
        c_all(step).wait_recv()
        drain = unfold(pick_dot(unpack, crecv[step].reshape(total, width)), parts)
        volts = [
            volts[x] + weight[x] * (moved[x] - STEP_DT * drain[x * cy : (x + 1) * cy])
            for x in range(cx)
        ]
        if step < STEPS - 1:
            if step > 0:
                send_rows(step + 1, volts)
                for d in range(1, blocks):
                    v_copy(step + 1, d).start()
            field = [weight[x] * volts[x] for x in range(cx)]
            stage(field, step + 1, True)
            start_halo(step + 1)

    phase_a = [weight[x] * (volts[x] - PHASE_REF) for x in range(cx)]
    stage(phase_a, STEPS + 1, False)
    start_halo(FINAL)
    for x in range(cx):
        volt_out[x] = volts[x]

    def with_length(a, b):
        return (a, b, jnp.sqrt(a * a + b * b))

    def each(change, point):
        return tuple(change(part) for part in point)

    zero_row = jnp.zeros((1, depth), jnp.float32)
    blank = lambda part: up_y(part, zero_row)
    points = [with_length(phase_a[x], phase_b[x]) for x in range(cx)]
    above = [each(up_z, p) for p in points]
    xz_a = {x: edge(points[x + 1], above[x]) for x in range(cx - 1)}
    xz_b = {x: edge(above[x], points[x - 1]) for x in range(1, cx)}
    wait_halo(LAG)
    wait_halo(FINAL)

    A, B = STEPS + 1, STEPS
    outer = [with_length(hx[A, e], hx[B, e]) for e in range(2)]
    rim = [with_length(hy[A, e], hy[B, e]) for e in range(2)]
    line = {-1: outer[0], cx: outer[1]}
    for x in range(cx):
        line[x] = points[x]

    def rows(xs, y):
        return tuple(jnp.concatenate([line[x][k][y : y + 1] for x in xs], axis=0) for k in range(3))

    yu = [tuple(up_y(points[x][k], rim[1][k][x : x + 1]) for k in range(3)) for x in range(cx)]
    yd = [tuple(down_y(points[x][k], rim[0][k][x : x + 1]) for k in range(3)) for x in range(cx)]
    below_row = each(lambda part: jnp.where(row_zlane == depth - 1, 0.0, wrap_up(part)), rim[0])
    over_row = each(lambda part: jnp.where(row_zlane == depth - 1, 0.0, wrap_up(part)), rim[1])

    xz_a[-1] = edge(line[0], each(up_z, line[-1]))
    xz_a[cx - 1] = edge(line[cx], above[cx - 1])
    xz_b[0] = edge(above[0], line[-1])
    xz_b[cx] = edge(each(up_z, line[cx]), line[cx - 1])

    yz_a = [edge(yu[x], above[x]) for x in range(cx)]
    yz_b = [edge(above[x], yd[x]) for x in range(cx)]
    yz_low = edge(rows(range(cx), 0), below_row)
    yz_high = edge(over_row, rows(range(cx), cy - 1))

    closed = {x: yu[x] for x in range(cx)}
    closed[-1], closed[cx] = each(blank, line[-1]), each(blank, line[cx])
    xy_a = {x: edge(line[x + 1], closed[x]) for x in range(-1, cx)}
    xy_b = {x: edge(closed[x], line[x - 1]) for x in range(cx + 1)}
    xy_low = edge(rim[0], rows(range(-1, cx - 1), 0))
    xy_high = edge(rows(range(1, cx + 1), 0), rim[0])

    for x in range(cx):
        charge[0, x] = (
            (xy_a[x] - down_y(xy_a[x - 1], xy_low[x : x + 1])) + (xy_b[x] - down_y(xy_b[x + 1], xy_high[x : x + 1]))
        )
        charge[1, x] = (
            (yz_a[x] + yz_b[x]) - down_z(down_y(yz_a[x], yz_low[x : x + 1]) + up_y(yz_b[x], yz_high[x : x + 1]))
        )
        charge[2, x] = (xz_a[x] + xz_b[x]) - down_z(xz_a[x - 1] + xz_b[x + 1])

    for which in range(EXCHANGES):
        wait_sent(which)
    cl_all().wait_send()
    for step in range(STEPS):
        v_all(step).wait_send()
        c_all(step).wait_send()


def write_out(volts, states, turns, volt_out, gates_out, charge, sems):
    copies = [
        pltpu.make_async_copy(src, dst, sems.at[i])
        for i, (src, dst) in enumerate(((states, gates_out), (turns, charge), (volts, volt_out)))
    ]
    for copy in copies:
        copy.start()
    for copy in copies:
        copy.wait()


def on_device(
    voltage, voltage_lag, tissue, fiber, conductivity, worker, gates,
    gate_half, gate_steep, gate_tmin, gate_tspan, channel,
):
    cx, cy, depth = voltage.shape
    gate_count, capacity, _ = gates.shape
    slabs, blocks = lax.axis_size("slab"), lax.axis_size("blk")
    pair = max(1, cx * cy // blocks)
    parts = max(1, min(8 // pair, depth // 128))
    width = depth // parts
    f32, i32 = jnp.float32, jnp.int32
    halos = STEPS + 2
    smem = pl.BlockSpec(memory_space=pltpu.SMEM)
    vmem = pl.BlockSpec(memory_space=pltpu.VMEM)
    dma = pltpu.SemaphoreType.DMA
    anywhere = pl.BlockSpec(memory_space=pl.ANY)
    held = pl.pallas_call(
        functools.partial(kernel, slabs, blocks, cx, cy, depth, gate_count, capacity, pair, parts),
        out_shape=(
            pltpu.VMEM(voltage.shape, f32),
            pltpu.VMEM(gates.shape, f32),
            pltpu.VMEM((3,) + voltage.shape, f32),
        ),
        in_specs=[smem] * 7 + [anywhere] * 5,
        out_specs=(vmem, vmem, vmem),
        scratch_shapes=[
            pltpu.VMEM(voltage.shape, f32),
            pltpu.VMEM(voltage.shape, f32),
            pltpu.VMEM(voltage.shape, i32),
            pltpu.VMEM(voltage.shape, i32),
            pltpu.VMEM(gates.shape, f32),
            pltpu.VMEM((halos, 2, cy, depth), f32),
            pltpu.VMEM((halos, 2, cx, depth), f32),
            pltpu.VMEM((STEPS, 4, 1, depth), f32),
            pltpu.VMEM((halos, 2, cy, depth), f32),
            pltpu.VMEM((halos, 2, cx, depth), f32),
            pltpu.VMEM((STEPS, 4, 1, depth), f32),
            pltpu.VMEM((2, 2, cy, depth), i32),
            pltpu.VMEM((2, 2, cx, depth), i32),
            pltpu.VMEM((2, 2, cx, depth), i32),
            pltpu.VMEM((STEPS, blocks, 8, width), f32),
            pltpu.VMEM((STEPS, blocks, 8, width), f32),
            pltpu.VMEM((STEPS, blocks, 8, width), f32),
            pltpu.VMEM((STEPS, blocks, 8, width), f32),
            pltpu.VMEM((blocks, 8, 128 + width), f32),
            pltpu.VMEM((blocks, 8, 128 + width), f32),
            pltpu.VMEM((6, cx, cy, depth), f32),
            pltpu.VMEM((3, cx + 1, cy, depth), f32),
            pltpu.VMEM((3, cx, cy, depth), f32),
            pltpu.VMEM((3, cx, cy, depth), f32),
            pltpu.VMEM((3, cx, cy, depth), f32),
            dma((5,)),
            dma((EXCHANGES, 8)), dma((EXCHANGES, 8)),
            dma((STEPS,)), dma((STEPS,)),
            dma((STEPS,)), dma((STEPS,)),
            dma, dma,
        ],
        compiler_params=pltpu.CompilerParams(collective_id=0, has_side_effects=True),
        name="steps",
    )(
        worker, conductivity, gate_half, gate_steep, gate_tmin, gate_tspan, channel,
        voltage, voltage_lag, tissue, fiber, gates,
    )
    return pl.pallas_call(
        write_out,
        out_shape=(
            jax.ShapeDtypeStruct(voltage.shape, f32),
            jax.ShapeDtypeStruct(gates.shape, f32),
            jax.ShapeDtypeStruct((3,) + voltage.shape, f32),
        ),
        in_specs=[vmem] * 3,
        out_specs=(anywhere,) * 3,
        scratch_shapes=[dma((3,))],
        name="write_out",
    )(*(pltpu.with_memory_space_constraint(x, pltpu.VMEM) for x in held))


def solution(mesh):
    grid = P("slab", "blk", None)
    in_specs = (
        grid, grid, grid, grid, P(), P("slab", "blk"), P(None, ("slab", "blk"), None),
        P(), P(), P(), P(), P(),
    )
    out_specs = (grid, P(None, ("slab", "blk"), None), P(None, "slab", "blk", None))
    return jax.shard_map(on_device, mesh=mesh, in_specs=in_specs, out_specs=out_specs, check_vma=False)
```

```python
import functools

import jax
import jax.numpy as jnp
from jax import lax
from jax.experimental import pallas as pl
from jax.experimental.pallas import tpu as pltpu
from jax.sharding import PartitionSpec as P

STEPS = 3
STEP_DT = 0.1
PHASE_REF = -0.2
PHASE_SOFT = 0.5
MESH = pl.DeviceIdType.MESH

FACES = ((-1, 0), (1, 0), (0, -1), (0, 1))
CORNERS = ((-1, -1), (-1, 1), (1, -1), (1, 1))
SIDES = FACES + CORNERS
TISSUE, FIBER, LAG, FINAL = STEPS, STEPS + 1, STEPS + 2, STEPS + 3
EXCHANGES = STEPS + 4


def pick_dot(onehot, values):
    first = values.astype(jnp.bfloat16)
    rest = values - first.astype(jnp.float32)
    second = rest.astype(jnp.bfloat16)
    third = (rest - second.astype(jnp.float32)).astype(jnp.bfloat16)
    dot = functools.partial(jnp.dot, preferred_element_type=jnp.float32)
    return dot(onehot, first) + dot(onehot, second) + dot(onehot, third)


def fold(x, parts):
    width = x.shape[1] // parts
    return jnp.concatenate([x[:, h * width : (h + 1) * width] for h in range(parts)], axis=0)


def unfold(x, parts):
    rows = x.shape[0] // parts
    return jnp.concatenate([x[h * rows : (h + 1) * rows] for h in range(parts)], axis=1)


def edge(p, q):
    cross = p[0] * q[1] - p[1] * q[0]
    den = p[2] * q[2] + (p[0] * q[0] + p[1] * q[1]) + PHASE_SOFT
    num = jnp.abs(cross)
    steep = num > 2.414213562373095 * den
    middle = num > 0.4142135623730950 * den
    top = jnp.where(steep, -den, jnp.where(middle, num - den, num))
    bottom = jnp.where(steep, num, jnp.where(middle, num + den, den))
    base = jnp.where(steep, 1.5707963267948966, jnp.where(middle, 0.7853981633974483, 0.0))
    x = top / bottom
    z = x * x
    poly = ((8.05374449538e-2 * z - 1.38776856032e-1) * z + 1.99777106478e-1) * z - 3.33329491539e-1
    angle = 2.0 * (base + (poly * z * x + x))
    return jnp.where(cross < 0.0, -angle, angle)


def kernel(
    slabs, blocks, cx, cy, depth, gate_count, capacity, pair, parts,
    worker_in, conductivity_in, half_in, steep_in, tmin_in, tspan_in, channel_in,
    voltage_in, lag_in, tissue_in, fiber_in, gates_in,
    volt_out, gates_out, charge,
    worker, conductivity, gate_half, gate_steep, gate_tmin, gate_tspan, channel,
    voltage, lag, tissue, fiber, gates,
    hx, hy, hc, sx, sy, sc, ix, iy, iys,
    vsend, vrecv, csend, crecv, clsend, clrecv, wsend, wrecv,
    sig, face_x, face_u, face_l, face_z,
    in_s, halo_ss, halo_rs, v_ss, v_rs, c_ss, c_rs, cl_ss, cl_rs, w_ss, w_rs,
):
    slab, blk = lax.axis_index("slab"), lax.axis_index("blk")
    tiles = cx * cy
    width = depth // parts
    loads = [
        pltpu.make_async_copy(src, dst, in_s.at[i])
        for i, (src, dst) in enumerate((
            (worker_in, worker), (voltage_in, voltage), (tissue_in, tissue), (fiber_in, fiber), (lag_in, lag),
            (conductivity_in, conductivity), (channel_in, channel), (half_in, gate_half), (steep_in, gate_steep),
            (tmin_in, gate_tmin), (tspan_in, gate_tspan), (gates_in, gates),
        ))
    ]

    def exists(side):
        dx, dy = side
        ok = None
        for cond in ([slab > 0] if dx < 0 else [slab < slabs - 1] if dx > 0 else []) + (
            [blk > 0] if dy < 0 else [blk < blocks - 1] if dy > 0 else []
        ):
            ok = cond if ok is None else jnp.logical_and(ok, cond)
        return ok

    def slot(refs, which, side):
        at = SIDES.index(side)
        return refs[0].at[which, at] if at < 2 else refs[1].at[which, at - 2] if at < 4 else refs[2].at[which, at - 4]

    def halo_copy(which, side, src, dst):
        dx, dy = side
        return pltpu.make_async_remote_copy(
            src_ref=src, dst_ref=dst,
            send_sem=halo_ss.at[which, SIDES.index(side)],
            recv_sem=halo_rs.at[which, SIDES.index((-dx, -dy))],
            device_id=(slab + dx, blk + dy), device_id_type=MESH,
        )

    def ring_copy(src, dst, ss, rs, to):
        return pltpu.make_async_remote_copy(
            src_ref=src, dst_ref=dst, send_sem=ss, recv_sem=rs,
            device_id=(slab, to), device_id_type=MESH,
        )

    def ends(which, side):
        opposite = (-side[0], -side[1])
        if which < STEPS or which == FINAL or which == LAG:
            at = which if which < STEPS else STEPS + (which - LAG)
            return slot((sx, sy, sc), at, side), slot((hx, hy, hc), at, opposite)
        ref = tissue if which == TISSUE else fiber
        at = which - TISSUE
        if side[0] != 0:
            return ref.at[0 if side[0] < 0 else cx - 1], slot((ix, iy), at, opposite)
        return iys.at[at, SIDES.index(side) - 2], slot((ix, iy), at, opposite)

    def sides_of(which):
        return SIDES if which < STEPS else FACES

    def start_halo(which):
        for side in sides_of(which):
            @pl.when(exists(side))
            def _():
                halo_copy(which, side, *ends(which, side)).start()

    def wait_halo(which):
        for side in sides_of(which):
            @pl.when(exists(side))
            def _():
                opposite = (-side[0], -side[1])
                src, dst = ends(which, opposite)
                dx, dy = side
                pltpu.make_async_remote_copy(
                    src_ref=src, dst_ref=dst,
                    send_sem=halo_ss.at[which, SIDES.index(side)],
                    recv_sem=halo_rs.at[which, SIDES.index(side)],
                    device_id=(slab + dx, blk + dy), device_id_type=MESH,
                ).wait_recv()

    def wait_sent(which):
        for side in sides_of(which):
            @pl.when(exists(side))
            def _():
                halo_copy(which, side, *ends(which, side)).wait_send()

    for side in SIDES:
        @pl.when(jnp.logical_not(exists(side)))
        def _():
            at = SIDES.index(side)
            ref = hx if at < 2 else hy if at < 4 else hc
            for which in range(STEPS + 2 if at < 4 else STEPS):
                ref[which, at % 2 if at < 4 else at - 4] = jnp.zeros(ref.shape[2:], jnp.float32)
            if at < 4:
                ints = ix if at < 2 else iy
                for which in range(2):
                    ints[which, at % 2] = jnp.zeros(ints.shape[2:], jnp.int32)

    paired = blocks & (blocks - 1) == 0
    powers = [1 << b for b in range(blocks.bit_length() - 1)]

    def partner(d, back=False):
        if not paired:
            return lax.rem(blk + (blocks - d if back else d), blocks)
        to = blk
        for power in powers:
            if d & power:
                to = to + power - 2 * power * lax.rem(blk // power, 2)
        return to

    far_first = sorted(range(1, blocks), key=lambda d: (-bin(d // 2).count("1"), d % 2, d))

    barrier = pltpu.get_barrier_semaphore()
    for d in range(1, blocks):
        pl.semaphore_signal(barrier, inc=1, device_id=(slab, partner(d)), device_id_type=MESH)
    expected = blocks - 1
    for side in SIDES:
        if side[0] != 0:
            there = exists(side)
            @pl.when(there)
            def _():
                pl.semaphore_signal(barrier, inc=1, device_id=(slab + side[0], blk + side[1]), device_id_type=MESH)
            expected = expected + there.astype(jnp.int32)

    for load in loads:
        load.start()

    loads[0].wait()
    total = blocks * 8
    cols = parts * tiles
    row_iota = lambda shape: lax.broadcasted_iota(jnp.int32, shape, 0)
    lane_iota = lambda shape: lax.broadcasted_iota(jnp.int32, shape, 1)
    lane = lane_iota((1, cols))
    tile_of = lax.rem(lane, tiles)
    part_of = lane // tiles
    target = jnp.zeros((1, cols), jnp.int32)
    for t in range(tiles):
        target = jnp.where(tile_of == t, worker[t // cy, t % cy], target)
    live = target >= 0
    holder = jnp.where(live, target // capacity, -1)
    own_holder = jnp.where(live, target // capacity, 0)
    own_row = jnp.where(live, lax.rem(target, capacity), 0)

    def to_col(row, size):
        square = jnp.broadcast_to(row, (size, size)).astype(jnp.float32)
        same = row_iota((size, size)) == lane_iota((size, size))
        return jnp.sum(jnp.where(same, square, 0.0), axis=1, keepdims=True).astype(jnp.int32)

    holder_col = to_col(holder, cols)[:tiles]
    earlier = (
        (jnp.broadcast_to(holder_col, (tiles, cols)) == jnp.broadcast_to(holder, (tiles, cols)))
        & (row_iota((tiles, cols)) < jnp.broadcast_to(tile_of, (tiles, cols)))
    )
    order = jnp.sum(jnp.where(earlier, 1.0, 0.0), axis=0, keepdims=True).astype(jnp.int32)
    if paired:
        ring = jnp.zeros_like(holder)
        for power in powers:
            mine, theirs = lax.rem(blk // power, 2), lax.rem(own_holder // power, 2)
            ring = ring + power * (mine + theirs - 2 * mine * theirs)
    else:
        ring = lax.rem(holder - blk + blocks, blocks)
    code = jnp.where(live, ring * 8 + part_of * pair + order, -1)
    pack_mask = row_iota((total, cols)) == jnp.broadcast_to(code, (total, cols))
    pack = jnp.where(pack_mask, 1.0, 0.0).astype(jnp.bfloat16)
    code_col = to_col(code, cols)
    unpack = jnp.where(jnp.broadcast_to(code_col, (cols, total)) == lane_iota((cols, total)), 1.0, 0.0).astype(jnp.bfloat16)
    row_code = jnp.broadcast_to((part_of * capacity + own_row + 1).astype(jnp.float32), (total, cols))
    claim_col = jnp.sum(jnp.where(pack_mask, row_code, 0.0), axis=1, keepdims=True) - 1.0
    clsend[...] = jnp.broadcast_to(claim_col, (total, 128)).reshape(blocks, 8, 128)

    loads[1].wait()
    loads[2].wait()
    weight = [tissue[x].astype(jnp.float32) for x in range(cx)]
    volts = [voltage[x] for x in range(cx)]

    def send_rows(step, planes):
        slots = pick_dot(pack, fold(jnp.concatenate(planes, axis=0), parts))
        vsend[step] = slots.reshape(blocks, 8, width)
        vrecv[step, 0] = slots[:8]

    def v_copy(step, d):
        return ring_copy(vsend.at[step, d], vrecv.at[step, d], v_ss.at[step], v_rs.at[step], partner(d))

    def c_copy(step, d):
        return ring_copy(csend.at[step, d], crecv.at[step, d], c_ss.at[step], c_rs.at[step], partner(d, True))

    def cl_copy(d):
        return ring_copy(clsend.at[d], clrecv.at[d], cl_ss, cl_rs, partner(d))

    def w_copy(d):
        return ring_copy(wsend.at[d], wrecv.at[d], w_ss, w_rs, partner(d))

    rest = pl.ds(1, blocks - 1)
    after = partner(1)

    def v_all(step):
        return ring_copy(vsend.at[step, rest], vrecv.at[step, rest], v_ss.at[step], v_rs.at[step], after)

    def c_all(step):
        return ring_copy(csend.at[step, rest], crecv.at[step, rest], c_ss.at[step], c_rs.at[step], after)

    def w_all():
        return ring_copy(wsend.at[rest], wrecv.at[rest], w_ss, w_rs, after)

    def cl_all():
        return ring_copy(clsend.at[rest], clrecv.at[rest], cl_ss, cl_rs, after)

    def stage(planes, at, corners):
        sx[at, 0] = planes[0]
        sx[at, 1] = planes[cx - 1]
        for end, y in ((0, 0), (1, cy - 1)):
            sy[at, end] = jnp.concatenate([planes[x][y : y + 1] for x in range(cx)], axis=0)
        if corners:
            for i, (dx, dy) in enumerate(CORNERS):
                y = 0 if dy < 0 else cy - 1
                sc[at, i] = planes[0 if dx < 0 else cx - 1][y : y + 1]

    send_rows(0, volts)
    bit_rows = fold(jnp.concatenate(weight, axis=0), parts).astype(jnp.bfloat16)
    wsend[...] = jnp.dot(pack, bit_rows, preferred_element_type=jnp.float32).reshape(blocks, 8, width)
    wrecv[0] = wsend[0]
    clrecv[0] = clsend[0]
    field = [weight[x] * volts[x] for x in range(cx)]
    stage(field, 0, True)
    loads[3].wait()
    for at, ref in ((0, tissue), (1, fiber)):
        for end, y in ((0, 0), (1, cy - 1)):
            iys[at, end] = jnp.concatenate([ref[x, y : y + 1] for x in range(cx)], axis=0)

    pl.semaphore_wait(barrier, expected)
    for d in far_first:
        cl_copy(d).start()
        v_copy(0, d).start()
    start_halo(0)
    start_halo(TISSUE)
    start_halo(FIBER)
    for d in far_first:
        w_copy(d).start()
    loads[4].wait()
    phase_b = [weight[x] * (lag[x] - PHASE_REF) for x in range(cx)]
    stage(phase_b, STEPS, False)
    start_halo(LAG)

    plane = (cy, depth)
    sub = lax.broadcasted_iota(jnp.int32, plane, 0)
    zlane = lax.broadcasted_iota(jnp.int32, plane, 1)
    row_zlane = lax.broadcasted_iota(jnp.int32, (cx, depth), 1)

    def up_y(x, row):
        return jnp.where(sub == cy - 1, jnp.broadcast_to(row, plane), pltpu.roll(x, cy - 1, 0))

    def down_y(x, row):
        return jnp.where(sub == 0, jnp.broadcast_to(row, plane), pltpu.roll(x, 1, 0))

    def wrap_up(x):
        return pltpu.roll(x, depth - 1, 1)

    def wrap_down(x):
        return pltpu.roll(x, 1, 1)

    def up_z(x):
        return jnp.where(zlane == depth - 1, 0.0, wrap_up(x))

    def down_z(x):
        return jnp.where(zlane == 0, 0.0, wrap_down(x))

    for load in loads[5:-1]:
        load.wait()

    def sigma(classes, component):
        table = [conductivity[component, i] for i in range(conductivity.shape[1])]
        out = jnp.full(classes.shape, table[0], jnp.float32)
        for i in range(1, len(table)):
            out = jnp.where(classes == i, table[i], out)
        return out

    names = ("x", "y", "z", "xy", "xz", "yz")

    def place(spots, d):
        others = [c for c in spots if c != d]
        return "xyz".index(others[0] if others else d)

    def scale(spots):
        return 0.5 if len(spots) == 1 else 0.125

    for component, spots in enumerate(names):
        own = [sigma(fiber[x], component) for x in range(cx)]
        for x in range(cx):
            sig[component, x] = own[x]
        if "x" in spots:
            for x in range(1, cx):
                face_x[place(spots, "x"), x] = scale(spots) * (own[x - 1] + own[x]) * (weight[x - 1] * weight[x])
        if "z" in spots:
            for x in range(cx):
                face_z[place(spots, "z"), x] = scale(spots) * (own[x] + wrap_up(own[x])) * (weight[x] * up_z(weight[x]))

    def outer_faces():
        w_lo, w_hi = ix[0, 0].astype(jnp.float32), ix[0, 1].astype(jnp.float32)
        wy_lo, wy_hi = iy[0, 0].astype(jnp.float32), iy[0, 1].astype(jnp.float32)
        both_u = [weight[x] * up_y(weight[x], wy_hi[x : x + 1]) for x in range(cx)]
        both_l = [weight[x] * down_y(weight[x], wy_lo[x : x + 1]) for x in range(cx)]
        for component, spots in enumerate(names):
            if "x" in spots:
                at = place(spots, "x")
                face_x[at, 0] = scale(spots) * (sigma(ix[1, 0], component) + sig[component, 0]) * (w_lo * weight[0])
                face_x[at, cx] = scale(spots) * (sig[component, cx - 1] + sigma(ix[1, 1], component)) * (weight[cx - 1] * w_hi)
            if "y" in spots:
                at = place(spots, "y")
                low, high = sigma(iy[1, 0], component), sigma(iy[1, 1], component)
                for x in range(cx):
                    mine = sig[component, x]
                    face_u[at, x] = scale(spots) * (mine + up_y(mine, high[x : x + 1])) * both_u[x]
                    face_l[at, x] = scale(spots) * (mine + down_y(mine, low[x : x + 1])) * both_l[x]

    def spread(field, step):
        f0 = [hx[step, 0]] + field + [hx[step, 1]]
        y_lo, y_hi = hy[step, 0], hy[step, 1]
        rows_lo = [hc[step, 0]] + [y_lo[x : x + 1] for x in range(cx)] + [hc[step, 2]]
        rows_hi = [hc[step, 1]] + [y_hi[x : x + 1] for x in range(cx)] + [hc[step, 3]]
        fu = [up_y(f0[i], rows_hi[i]) for i in range(cx + 2)]
        fd = [down_y(f0[i], rows_lo[i]) for i in range(cx + 2)]
        dy = [fu[i] - fd[i] for i in range(cx + 2)]
        up0 = [up_z(f) for f in f0]
        dz = [up0[i] - down_z(f0[i]) for i in range(cx + 2)]
        z_lo, z_hi = {}, {}
        flux_x = [
            face_x[0, i] * (f0[i + 1] - f0[i]) + face_x[1, i] * (dy[i] + dy[i + 1]) + face_x[2, i] * (dz[i] + dz[i + 1])
            for i in range(cx + 1)
        ]
        result = []
        for x in range(cx):
            i = x + 1
            dx, dxu, dxd = f0[i + 1] - f0[i - 1], fu[i + 1] - fu[i - 1], fd[i + 1] - fd[i - 1]
            dzu, dzd = up_z(fu[i]) - down_z(fu[i]), up_z(fd[i]) - down_z(fd[i])
            flux_u = face_u[1, x] * (fu[i] - f0[i]) + face_u[0, x] * (dx + dxu) + face_u[2, x] * (dz[i] + dzu)
            flux_l = face_l[1, x] * (f0[i] - fd[i]) + face_l[0, x] * (dx + dxd) + face_l[2, x] * (dz[i] + dzd)
            flux_z = (
                face_z[2, x] * (up0[i] - f0[i])
                + face_z[0, x] * (dx + wrap_up(dx))
                + face_z[1, x] * (dy[i] + wrap_up(dy[i]))
            )
            result.append((flux_x[i] - flux_x[i - 1]) + (flux_u - flux_l) + (flux_z - wrap_down(flux_z)))
        return result

    for step in range(STEPS):
        states = gates if step == 0 else gates_out
        if step == 0:
            v_all(0).wait_recv()
            cl_all().wait_recv()
            claims = clrecv[...].reshape(total, 128)
            picks = parts * capacity
            claim = claims[:, :1].astype(jnp.int32)
            give = jnp.where(jnp.broadcast_to(claim, (total, picks)) == lane_iota((total, picks)), 1.0, 0.0).astype(jnp.bfloat16)
            same = row_iota((total, total)) == lane_iota((total, total))
            claim_row = jnp.sum(
                jnp.where(same, jnp.broadcast_to(claims[:, :1], (total, total)), 0.0), axis=0, keepdims=True
            ).astype(jnp.int32)
            take = jnp.where(row_iota((picks, total)) == jnp.broadcast_to(claim_row, (picks, total)), 1.0, 0.0).astype(jnp.bfloat16)
            loads[-1].wait()
        else:
            v_all(step).wait_recv()
        if step == 1:
            w_all().wait_recv()
            bits = wrecv[...].reshape(total, width).astype(jnp.bfloat16)
            row_weight = unfold(jnp.dot(take, bits, preferred_element_type=jnp.float32), parts)
        arrived = unfold(pick_dot(take, vrecv[step].reshape(total, width)), parts)
        v = v + row_weight * (arrived - STEP_DT * current) if step == 1 else arrived
        s = [states[g] for g in range(12)]
        current = (
            channel[0] * s[0] * s[0] * s[0] * s[1] * s[2] * (v - 1.2)
            + channel[1] * s[3] * s[4] * s[5] * s[6] * (v - 1.0)
            + channel[2] * s[7] * s[8] * (v + 0.9)
            + channel[3] * s[9] * s[10] * (v + 0.9)
            + channel[4] * s[11] * s[11] * (v + 0.8)
            + channel[5] * (v + 0.9) / (1.0 + jnp.exp(4.0 * (v + 0.6)))
        )
        back = pick_dot(give, fold(current, parts))
        csend[step] = back.reshape(blocks, 8, width)
        crecv[step, 0] = back[:8]
        for d in far_first:
            c_copy(step, d).start()
        if step == 0:
            wait_halo(TISSUE)
            wait_halo(FIBER)
            outer_faces()
            wait_halo(0)
            moved = spread(field, 0)
            send_rows(1, moved)
            for d in far_first:
                v_copy(1, d).start()
        for g in range(gate_count):
            off = v - gate_half[g]
            goal = 1.0 / (1.0 + jnp.exp(-gate_steep[g] * off))
            quad = 1.0 + 4.0 * off * off
            decay = jnp.exp((-STEP_DT * quad) / (gate_tmin[g] * quad + gate_tspan[g]))
            gates_out[g] = goal + (states[g] - goal) * decay
        if step > 0:
            wait_halo(step)
            moved = spread(field, step)
        c_all(step).wait_recv()
        drain = unfold(pick_dot(unpack, crecv[step].reshape(total, width)), parts)
        volts = [
            volts[x] + weight[x] * (moved[x] - STEP_DT * drain[x * cy : (x + 1) * cy])
            for x in range(cx)
        ]
        if step < STEPS - 1:
            if step > 0:
                send_rows(step + 1, volts)
                for d in far_first:
                    v_copy(step + 1, d).start()
            field = [weight[x] * volts[x] for x in range(cx)]
            stage(field, step + 1, True)
            start_halo(step + 1)

    phase_a = [weight[x] * (volts[x] - PHASE_REF) for x in range(cx)]
    stage(phase_a, STEPS + 1, False)
    start_halo(FINAL)
    for x in range(cx):
        volt_out[x] = volts[x]

    def with_length(a, b):
        return (a, b, jnp.sqrt(a * a + b * b))

    def each(change, point):
        return tuple(change(part) for part in point)

    zero_row = jnp.zeros((1, depth), jnp.float32)
    blank = lambda part: up_y(part, zero_row)
    points = [with_length(phase_a[x], phase_b[x]) for x in range(cx)]
    above = [each(up_z, p) for p in points]
    xz_a = {x: edge(points[x + 1], above[x]) for x in range(cx - 1)}
    xz_b = {x: edge(above[x], points[x - 1]) for x in range(1, cx)}
    wait_halo(LAG)
    wait_halo(FINAL)

    A, B = STEPS + 1, STEPS
    outer = [with_length(hx[A, e], hx[B, e]) for e in range(2)]
    rim = [with_length(hy[A, e], hy[B, e]) for e in range(2)]
    line = {-1: outer[0], cx: outer[1]}
    for x in range(cx):
        line[x] = points[x]

    def rows(xs, y):
        return tuple(jnp.concatenate([line[x][k][y : y + 1] for x in xs], axis=0) for k in range(3))

    yu = [tuple(up_y(points[x][k], rim[1][k][x : x + 1]) for k in range(3)) for x in range(cx)]
    yd = [tuple(down_y(points[x][k], rim[0][k][x : x + 1]) for k in range(3)) for x in range(cx)]
    below_row = each(lambda part: jnp.where(row_zlane == depth - 1, 0.0, wrap_up(part)), rim[0])
    over_row = each(lambda part: jnp.where(row_zlane == depth - 1, 0.0, wrap_up(part)), rim[1])

    xz_a[-1] = edge(line[0], each(up_z, line[-1]))
    xz_a[cx - 1] = edge(line[cx], above[cx - 1])
    xz_b[0] = edge(above[0], line[-1])
    xz_b[cx] = edge(each(up_z, line[cx]), line[cx - 1])

    yz_a = [edge(yu[x], above[x]) for x in range(cx)]
    yz_b = [edge(above[x], yd[x]) for x in range(cx)]
    yz_low = edge(rows(range(cx), 0), below_row)
    yz_high = edge(over_row, rows(range(cx), cy - 1))

    closed = {x: yu[x] for x in range(cx)}
    closed[-1], closed[cx] = each(blank, line[-1]), each(blank, line[cx])
    xy_a = {x: edge(line[x + 1], closed[x]) for x in range(-1, cx)}
    xy_b = {x: edge(closed[x], line[x - 1]) for x in range(cx + 1)}
    xy_low = edge(rim[0], rows(range(-1, cx - 1), 0))
    xy_high = edge(rows(range(1, cx + 1), 0), rim[0])

    for x in range(cx):
        charge[0, x] = (
            (xy_a[x] - down_y(xy_a[x - 1], xy_low[x : x + 1])) + (xy_b[x] - down_y(xy_b[x + 1], xy_high[x : x + 1]))
        )
        charge[1, x] = (
            (yz_a[x] + yz_b[x]) - down_z(down_y(yz_a[x], yz_low[x : x + 1]) + up_y(yz_b[x], yz_high[x : x + 1]))
        )
        charge[2, x] = (xz_a[x] + xz_b[x]) - down_z(xz_a[x - 1] + xz_b[x + 1])

    for which in range(EXCHANGES):
        wait_sent(which)
    cl_all().wait_send()
    w_all().wait_send()
    for step in range(STEPS):
        v_all(step).wait_send()
        c_all(step).wait_send()


def write_out(volts, states, turns, volt_out, gates_out, charge, sems):
    copies = [
        pltpu.make_async_copy(src, dst, sems.at[i])
        for i, (src, dst) in enumerate(((states, gates_out), (turns, charge), (volts, volt_out)))
    ]
    for copy in copies:
        copy.start()
    for copy in copies:
        copy.wait()


def on_device(
    voltage, voltage_lag, tissue, fiber, conductivity, worker, gates,
    gate_half, gate_steep, gate_tmin, gate_tspan, channel,
):
    cx, cy, depth = voltage.shape
    gate_count, capacity, _ = gates.shape
    slabs, blocks = lax.axis_size("slab"), lax.axis_size("blk")
    pair = max(1, cx * cy // blocks)
    parts = max(1, min(8 // pair, depth // 128))
    width = depth // parts
    f32, i32 = jnp.float32, jnp.int32
    halos = STEPS + 2
    vmem = pl.BlockSpec(memory_space=pltpu.VMEM)
    dma = pltpu.SemaphoreType.DMA
    anywhere = pl.BlockSpec(memory_space=pl.ANY)
    held = pl.pallas_call(
        functools.partial(kernel, slabs, blocks, cx, cy, depth, gate_count, capacity, pair, parts),
        out_shape=(
            pltpu.VMEM(voltage.shape, f32),
            pltpu.VMEM(gates.shape, f32),
            pltpu.VMEM((3,) + voltage.shape, f32),
        ),
        in_specs=[anywhere] * 12,
        out_specs=(vmem, vmem, vmem),
        scratch_shapes=[
            pltpu.SMEM(worker.shape, i32),
            pltpu.SMEM(conductivity.shape, f32),
            pltpu.SMEM(gate_half.shape, f32),
            pltpu.SMEM(gate_steep.shape, f32),
            pltpu.SMEM(gate_tmin.shape, f32),
            pltpu.SMEM(gate_tspan.shape, f32),
            pltpu.SMEM(channel.shape, f32),
            pltpu.VMEM(voltage.shape, f32),
            pltpu.VMEM(voltage.shape, f32),
            pltpu.VMEM(voltage.shape, i32),
            pltpu.VMEM(voltage.shape, i32),
            pltpu.VMEM(gates.shape, f32),
            pltpu.VMEM((halos, 2, cy, depth), f32),
            pltpu.VMEM((halos, 2, cx, depth), f32),
            pltpu.VMEM((STEPS, 4, 1, depth), f32),
            pltpu.VMEM((halos, 2, cy, depth), f32),
            pltpu.VMEM((halos, 2, cx, depth), f32),
            pltpu.VMEM((STEPS, 4, 1, depth), f32),
            pltpu.VMEM((2, 2, cy, depth), i32),
            pltpu.VMEM((2, 2, cx, depth), i32),
            pltpu.VMEM((2, 2, cx, depth), i32),
            pltpu.VMEM((STEPS, blocks, 8, width), f32),
            pltpu.VMEM((STEPS, blocks, 8, width), f32),
            pltpu.VMEM((STEPS, blocks, 8, width), f32),
            pltpu.VMEM((STEPS, blocks, 8, width), f32),
            pltpu.VMEM((blocks, 8, 128), f32),
            pltpu.VMEM((blocks, 8, 128), f32),
            pltpu.VMEM((blocks, 8, width), f32),
            pltpu.VMEM((blocks, 8, width), f32),
            pltpu.VMEM((6, cx, cy, depth), f32),
            pltpu.VMEM((3, cx + 1, cy, depth), f32),
            pltpu.VMEM((3, cx, cy, depth), f32),
            pltpu.VMEM((3, cx, cy, depth), f32),
            pltpu.VMEM((3, cx, cy, depth), f32),
            dma((12,)),
            dma((EXCHANGES, 8)), dma((EXCHANGES, 8)),
            dma((STEPS,)), dma((STEPS,)),
            dma((STEPS,)), dma((STEPS,)),
            dma, dma, dma, dma,
        ],
        compiler_params=pltpu.CompilerParams(collective_id=0, has_side_effects=True),
        name="steps",
    )(
        worker, conductivity, gate_half, gate_steep, gate_tmin, gate_tspan, channel,
        voltage, voltage_lag, tissue, fiber, gates,
    )
    return pl.pallas_call(
        write_out,
        out_shape=(
            jax.ShapeDtypeStruct(voltage.shape, f32),
            jax.ShapeDtypeStruct(gates.shape, f32),
            jax.ShapeDtypeStruct((3,) + voltage.shape, f32),
        ),
        in_specs=[vmem] * 3,
        out_specs=(anywhere,) * 3,
        scratch_shapes=[dma((3,))],
        name="write_out",
    )(*(pltpu.with_memory_space_constraint(x, pltpu.VMEM) for x in held))


def solution(mesh):
    grid = P("slab", "blk", None)
    in_specs = (
        grid, grid, grid, grid, P(), P("slab", "blk"), P(None, ("slab", "blk"), None),
        P(), P(), P(), P(), P(),
    )
    out_specs = (grid, P(None, ("slab", "blk"), None), P(None, "slab", "blk", None))
    return jax.shard_map(on_device, mesh=mesh, in_specs=in_specs, out_specs=out_specs, check_vma=False)
```
